256 devices in a mesh: tm: 32 (over z_lo, x, core), freq: 8 (over z_hi, y).
Axes of the slice: x: 4, y: 4, z: 8 (z_hi: 2, z_lo: 4; z = z_hi * 4 + z_lo), core: 2. Of those that a mesh axis runs over, the one named last changes fastest.
Arguments:
- visibilities: float32 [32, 8, 8, 512], P('tm', 'freq'), may hold values from -6 to 6
- coherency: bfloat16 [32, 8, 8, 64, 512], P('tm', 'freq'), may hold values from -0.75 to 0.75
- stations: int32 [32, 2, 512], P('tm'), may hold values from 0 to 511, as said below
- jones: float32 [8, 8, 32768], P('freq', None, 'tm'), may hold values from -3 to 3
- dual: float32 [8, 8, 32768], P('freq', None, 'tm'), may hold values from -1.8 to 1.8
- cluster: int32 [64], replicated, may hold values from 0 to 7
- rho_table: float32 [8], replicated, may hold values from 0.3 to 3
Outputs:
- jones_out: float32 [8, 8, 32768], P('freq', None, 'tm')
- dual_out: float32 [8, 8, 32768], P('freq', None, 'tm')
- consensus: float32 [3, 8, 32768], P(None, None, 'tm')
The draws below stay inside these ranges and needn't reach their ends.
Inputs may be any that keep to these rules, and one draw needn't show every extreme that they name: Each baseline joins two different stations.
All inputs are finite; a program needn't handle non-finite values.
Results may differ from the reference program's by a relative error of at most 0.0003.
Values may be sent and summed in bfloat16 or wider, within the bound.
No kernel may reach another device: no remote copies, remote signals or barrier semaphores. Data moves between devices by JAX's collectives and lax.ppermute only.
A program may use at most 64 MiB of HBM per device.

```python
import math
import jax
import jax.numpy as jnp
import numpy as np
from jax import lax

S = 512
K = 64
NCL = 8
BL_DEV = 512
ITERS = 2
TIMES = 32
NCH = 8
NP = 3


def draw_stations(key, part):
    key_first, key_offset = jax.random.split(jax.random.fold_in(key, 11))
    first_st = jax.random.randint(key_first, (TIMES, BL_DEV), 0, S)
    offsets = jax.random.randint(key_offset, (TIMES, BL_DEV), 1, S)
    second_st = (first_st + offsets) % S
    leading = jnp.arange(BL_DEV)[None, :] == 0
    first_st = jnp.where(leading, 0, first_st)
    second_st = jnp.where(leading, S - 1, second_st)
    return jnp.stack([first_st, second_st], axis=1).astype(jnp.int32)


def draw_jones(key, part):
    inner_key = jax.random.fold_in(key, 23)
    direction = (jnp.arange(K * S) // S).astype(jnp.float32)
    spread = 0.4 + 0.8 * direction / (K - 1)
    values = jnp.clip(jax.random.normal(inner_key, (NCH, 8, K * S), jnp.float32), -2.5, 2.5)
    return (values * spread[None, None, :]).astype(jnp.float32)


def plant(values, rng, smallest, top_value):
    spot = [jax.random.randint(jax.random.fold_in(rng, axis), (), 0, length) for axis, length in enumerate(values.shape)]
    longest = values.shape.index(max(values.shape))
    neighbour = spot[:longest] + [(spot[longest] + 1) % values.shape[longest]] + spot[longest + 1:]
    return values.at[tuple(spot)].set(smallest).at[tuple(neighbour)].set(top_value)


def block_levels(key, shape, shards, low, top_value):
    def one(dim, parts):
        draws = jax.random.uniform(jax.random.fold_in(jax.random.fold_in(key, 6), dim), (parts,), jnp.float32, low / len(shards), top_value / len(shards))
        return jnp.repeat(jnp.exp(draws), shape[dim] // parts).reshape((-1,) + (1,) * (len(shape) - dim - 1))

    factor_of = one(*shards[0])
    for cut in shards[1:]:
        factor_of = factor_of * one(*cut)
    return factor_of


def scatter_about(own_key, shape, scale, most, pieces=(), kind=jnp.bfloat16):
    drawn = jax.random.normal(own_key, shape, jnp.float32) * scale
    if len(pieces) > 0:
        drawn = block_levels(own_key, shape, pieces, -0.22, 0.18) * drawn
    return jnp.clip(drawn, min=-most, max=most).astype(kind)


def setup_inputs(seed: int = 0) -> dict:
    streams_of = jax.random.split(jax.random.key(seed), 8)
    return {
        "visibilities": scatter_about(streams_of[0], (TIMES, NCH, 8, BL_DEV), 1.0, 6.0, ((0, 32), (1, 8)), jnp.float32),
        "coherency": scatter_about(streams_of[1], (TIMES, NCH, 8, K, BL_DEV), 0.125, 0.75, ((0, 32), (1, 8))),
        "stations": draw_stations(jax.random.fold_in(streams_of[7], 71), 0),
        "jones": draw_jones(jax.random.fold_in(streams_of[7], 71), 0),
        "dual": scatter_about(streams_of[4], (NCH, 8, K * S), 0.3, 1.8, ((0, 8), (2, 32)), jnp.float32),
        "cluster": plant(jax.random.randint(streams_of[5], (K,), 0, NCL), jax.random.fold_in(streams_of[5], 1), 0, NCL - 1).astype(jnp.int32),
        "rho_table": jnp.clip(jnp.exp(jax.random.uniform(streams_of[6], (NCL,), jnp.float32, math.log(0.3), math.log(3.0))), 0.3, 3.0),
    }


step_size = 0.5
epsilon = 1e-06
highest = lax.Precision.HIGHEST

def poly_basis(channels, degrees):
    points = np.linspace(-1.0, 1.0, channels)
    columns = []
    for degree in range(degrees):
        column = points ** degree
        for earlier in columns:
            column = column - np.dot(earlier, column) * earlier
        column = column / np.sqrt(np.dot(column, column))
        columns.append(column)
    return np.stack(columns, axis=1).astype(np.float32)

def split_entries(stacked):
    return [[(stacked[4 * left_index + 2 * right_index], stacked[4 * left_index + 2 * right_index + 1]) for right_index in range(2)] for left_index in range(2)]

def times_pair(left_val, right_val):
    return (left_val[0] * right_val[0] - left_val[1] * right_val[1], left_val[0] * right_val[1] + left_val[1] * right_val[0])

def times_conj(left_val, right_val):
    return (left_val[0] * right_val[0] + left_val[1] * right_val[1], left_val[1] * right_val[0] - left_val[0] * right_val[1])

def add_pairs(left_val, right_val):
    return (left_val[0] + right_val[0], left_val[1] + right_val[1])

def direction_model(first_gain, sky_model, second_gain):
    first_mat = split_entries(first_gain)
    sky_mat = split_entries(sky_model)
    second_mat = split_entries(second_gain)
    product = [[add_pairs(times_pair(first_mat[left_index][0], sky_mat[0][right_index]), times_pair(first_mat[left_index][1], sky_mat[1][right_index])) for right_index in range(2)] for left_index in range(2)]
    result = [[add_pairs(times_conj(product[left_index][0], second_mat[right_index][0]), times_conj(product[left_index][1], second_mat[right_index][1])) for right_index in range(2)] for left_index in range(2)]
    components = []
    for left_index in range(2):
        for right_index in range(2):
            components.append(result[left_index][right_index][0])
            components.append(result[left_index][right_index][1])
    return jnp.stack(components, axis=0)

def model_sum(gain_block, first_station, second_station, sky_model):
    first_gain = jnp.take(gain_block, first_station, axis=2)
    second_gain = jnp.take(gain_block, second_station, axis=2)
    return lax.optimization_barrier(jnp.sum(direction_model(first_gain, sky_model, second_gain), axis=1))

def gradient_all(jones, visibilities, coherency, stations):
    gain_blocks = jones.reshape(NCH, 8, K, S)
    weight = np.sqrt(S / (2.0 * TIMES * BL_DEV)).astype(np.float32)

    def per_time(running, inputs):
        vis_slot, coh_slot, pair_slot = inputs

        def per_channel(gain_block, vis_chan, coh_chan):
            model_vis, pullback = jax.vjp(lambda gains: model_sum(gains, pair_slot[0], pair_slot[1], coh_chan.astype(jnp.float32)), gain_block)
            return pullback(-weight * (vis_chan - model_vis))[0]
        return (running + jax.vmap(per_channel)(gain_blocks, vis_slot, coh_slot), None)
    running, _ = lax.scan(per_time, jnp.zeros((NCH, 8, K, S), jnp.float32), (visibilities, coherency, stations))
    return running.reshape(NCH, 8, K * S)

def reference(visibilities, coherency, stations, jones, dual, cluster, rho_table):
    rho_dir = lax.optimization_barrier(jnp.sum(jnp.where(cluster[:, None] == jnp.arange(NCL, dtype=jnp.int32)[None, :], rho_table[None, :], jnp.float32(0.0)), axis=1))
    rho_flat = jnp.repeat(rho_dir, S)
    poly_table = jnp.asarray(poly_basis(NCH, NP))

    def consensus_of(state, dual_now):
        return jnp.einsum('fj,fcn->jcn', poly_table, state + dual_now / rho_flat, precision=highest)

    def project(poly_coef):
        return jnp.einsum('fj,jcn->fcn', poly_table, poly_coef, precision=highest)
    poly_coef = consensus_of(jones, dual)
    fitted = project(poly_coef)
    for iteration in range(ITERS):
        gradient = gradient_all(jones, visibilities, coherency, stations)
        descent = gradient + dual + rho_flat * (jones - fitted)
        scale = jnp.sqrt(lax.optimization_barrier(jnp.mean(descent * descent, axis=(1, 2), keepdims=True)) + epsilon)
        jones = jones - step_size * descent / scale
        poly_coef = consensus_of(jones, dual)
        fitted = project(poly_coef)
        dual = dual + rho_flat * (jones - fitted)
    return (jones, dual, poly_coef)
```

```python
import functools
import math

import jax
import jax.numpy as jnp
import numpy as np
from jax import lax
from jax.experimental import pallas as pl
from jax.experimental.pallas import tpu as pltpu
from jax.sharding import PartitionSpec as P

S = 512
K = 64
ITERS = 2
step_size = 0.5
epsilon = 1e-06


f32 = jnp.float32
bf16 = jnp.bfloat16


def poly_basis(channels, degrees):
    points = np.linspace(-1.0, 1.0, channels)
    columns = []
    for degree in range(degrees):
        column = points**degree
        for earlier in columns:
            column = column - np.dot(earlier, column) * earlier
        column = column / np.sqrt(np.dot(column, column))
        columns.append(column)
    return np.stack(columns, axis=1).astype(np.float32)


def swap(value, axis, mask):
    size = 32 if axis == "tm" else 8
    return lax.ppermute(value, axis, [(i, i ^ mask) for i in range(size)])


def spread_over_tm(value):
    parts = [value] + [swap(value, "tm", 8 * d) for d in (1, 2, 3)]
    line = jnp.stack(parts)
    parts = [line] + [swap(line, "tm", 2 * d) for d in (1, 2, 3)]
    own = jnp.stack(parts).reshape(1024, 128)
    return own, swap(own, "tm", 1)


def sum_over_tm(own, other):
    half = (own + swap(other, "tm", 1)).reshape(4, 4, 64, 128)
    line = half[0] + swap(half[1], "tm", 2)
    line = line + (swap(half[2], "tm", 4) + swap(half[3], "tm", 6))
    return (line[0] + swap(line[1], "tm", 8)) + (swap(line[2], "tm", 16) + swap(line[3], "tm", 24))


def pair_times(a, b):
    return (a[0] * b[0] - a[1] * b[1], a[0] * b[1] + a[1] * b[0])


def pair_times_conj(a, b):
    return (a[0] * b[0] + a[1] * b[1], a[1] * b[0] - a[0] * b[1])


def pair_conj_times(a, b):
    return (a[0] * b[0] + a[1] * b[1], a[0] * b[1] - a[1] * b[0])


def pair_add(a, b):
    return (a[0] + b[0], a[1] + b[1])


def matrix(parts):
    return [[(parts[0], parts[1]), (parts[2], parts[3])], [(parts[4], parts[5]), (parts[6], parts[7])]]


def flat(m):
    return [m[0][0][0], m[0][0][1], m[0][1][0], m[0][1][1], m[1][0][0], m[1][0][1], m[1][1][0], m[1][1][1]]


def times(a, b):
    return [[pair_add(pair_times(a[i][0], b[0][j]), pair_times(a[i][1], b[1][j])) for j in range(2)] for i in range(2)]


def times_h(a, b):
    return [
        [pair_add(pair_times_conj(a[i][0], b[j][0]), pair_times_conj(a[i][1], b[j][1])) for j in range(2)]
        for i in range(2)
    ]


def h_times(a, b):
    return [
        [pair_add(pair_conj_times(a[0][i], b[0][j]), pair_conj_times(a[1][i], b[1][j])) for j in range(2)]
        for i in range(2)
    ]


def split(value):
    high = value.astype(bf16)
    return high, (value - high.astype(f32)).astype(bf16)


def gradient_kernel(weight, count, moved, *refs):
    if moved:
        own, other, down, dother, sky, pick, place, vis, gown, gother, rate, lhs, gains, left, terms = refs
        total = jnp.zeros((64, 128), f32)
        for ref in (down, dother):
            for row in range(16):
                block = ref[row * 64 : row * 64 + 64, :]
                total = total + block * block
        mean = jnp.sum(total, axis=(0, 1), keepdims=True) / count
        step = step_size / jnp.sqrt(mean + epsilon)
        rate[...] = jnp.broadcast_to(step, (8, 128))
        step = jnp.broadcast_to(step, (16, 128))
    else:
        own, other, sky, pick, place, vis, gown, gother, lhs, gains, left, terms = refs
        down = dother = None
    for half, (ref, dref) in enumerate(((own, down), (other, dother))):
        for c in range(8):
            for block in range(8):
                rows = pl.ds(block * 8 + c, 16, stride=64)
                value = ref[rows, :]
                if moved:
                    value = value - step * dref[rows, :]
                high, low = split(value)
                row = c * 64 + block // 4 * 32 + half * 16
                lane = block % 4 * 128
                lhs[row : row + 16, lane : lane + 128] = high
                lhs[row : row + 16, 512 + lane : 640 + lane] = low
    gains[...] = jnp.dot(lhs[...], pick[...], preferred_element_type=f32)

    for nb in range(4):
        lanes = slice(nb * 128, nb * 128 + 128)
        qlanes = slice(512 + nb * 128, 512 + nb * 128 + 128)

        def forward(kb, acc, lanes=lanes, qlanes=qlanes):
            def rows(c):
                return pl.ds(pl.multiple_of(c * 64 + kb * 8, 8), 8)

            first = matrix([gains[rows(c), lanes] for c in range(8)])
            second = matrix([gains[rows(c), qlanes] for c in range(8)])
            model = matrix([sky[rows(c), lanes] for c in range(8)])
            product = times(first, model)
            for c, value in enumerate(flat(product)):
                left[rows(c), lanes] = value
            result = flat(times_h(product, second))
            return tuple(a + r for a, r in zip(acc, result))

        acc = lax.fori_loop(0, 8, forward, tuple(jnp.zeros((8, 128), f32) for _ in range(8)))
        errors = []
        for c in range(8):
            model = jnp.sum(acc[c], axis=0, keepdims=True)
            errors.append(jnp.broadcast_to(-weight * (vis[c : c + 1, lanes] - model), (8, 128)))
        errors = matrix(errors)

        def backward(kb, carry, lanes=lanes, qlanes=qlanes, errors=errors):
            def rows16(c):
                return pl.ds(pl.multiple_of(c * 64 + kb * 16, 16), 16)

            out_p, out_q = [], []
            for part in range(2):
                def rows(c, part=part):
                    return pl.ds(pl.multiple_of(c * 64 + kb * 16 + part * 8, 8), 8)

                second = matrix([gains[rows(c), qlanes] for c in range(8)])
                model = matrix([sky[rows(c), lanes] for c in range(8)])
                product = matrix([left[rows(c), lanes] for c in range(8)])
                right = times_h(second, model)
                out_p.append(flat(times(errors, right)))
                out_q.append(flat(h_times(errors, product)))
            for c in range(8):
                high, low = split(jnp.concatenate([out_p[0][c], out_p[1][c]], axis=0))
                terms[rows16(c), lanes] = high
                terms[rows16(c), slice(1024 + lanes.start, 1024 + lanes.stop)] = low
                high, low = split(jnp.concatenate([out_q[0][c], out_q[1][c]], axis=0))
                terms[rows16(c), qlanes] = high
                terms[rows16(c), slice(1024 + qlanes.start, 1024 + qlanes.stop)] = low
            return carry

        lax.fori_loop(0, 4, backward, 0)

    gains[:, 0:512] = jnp.dot(terms[...], place[...], preferred_element_type=f32)
    for half, ref in enumerate((gown, gother)):
        for c in range(8):
            for block in range(8):
                row = c * 64 + block // 4 * 32 + half * 16
                lane = block % 4 * 128
                ref[pl.ds(block * 8 + c, 16, stride=64), :] = gains[row : row + 16, lane : lane + 128]


def gradient(weight, own, other, sky, pick, place, vis, moves=None):
    vmem = pl.BlockSpec(memory_space=pltpu.VMEM)
    shape = jax.ShapeDtypeStruct((1024, 128), f32)
    outs = [shape, shape] + ([jax.ShapeDtypeStruct((8, 128), f32)] if moves else [])
    args = (own, other) + (moves or ()) + (sky, pick, place, vis)
    return pl.pallas_call(
        functools.partial(gradient_kernel, weight, 8.0 * K * S, moves is not None),
        out_shape=outs,
        in_specs=[vmem] * len(args),
        out_specs=[vmem] * len(outs),
        scratch_shapes=[
            pltpu.VMEM((512, 1024), bf16),
            pltpu.VMEM((512, 1024), f32),
            pltpu.VMEM((512, 512), f32),
            pltpu.VMEM((512, 2048), bf16),
        ],
        compiler_params=pltpu.CompilerParams(vmem_limit_bytes=40 << 20),
        name="gradient_moved" if moves else "gradient_start",
    )(*args)


def body(visibilities, coherency, stations, jones, dual, cluster, rho_table):
    channels = lax.axis_size("freq")
    degrees = min(3, channels - 1)
    tm = lax.axis_index("tm")
    freq = lax.axis_index("freq")
    weight = np.float32(math.sqrt(S / (2.0 * lax.axis_size("tm") * visibilities.shape[3])))

    def packed(value):
        return value.reshape(8, 8, 128).transpose(1, 0, 2).reshape(64, 128)

    def unpacked(value):
        return value.reshape(-1, 8, 8, 128).transpose(0, 2, 1, 3).reshape(-1, 8, 1024)

    start = packed(jones[0])
    dual_now = packed(dual[0])

    rho_dir = jnp.sum(
        jnp.where(cluster[:, None] == jnp.arange(rho_table.shape[0], dtype=jnp.int32)[None, :], rho_table[None, :], 0.0),
        axis=1,
    )
    rho = jnp.repeat(lax.dynamic_slice_in_dim(rho_dir, tm * 2, 2), 32)[:, None]
    table = jnp.asarray(poly_basis(channels, degrees))
    basis = [lax.dynamic_index_in_dim(table, freq ^ d, 0, keepdims=False) for d in range(4)]

    def consensus_of(value):
        parts = [value] + [swap(value, "freq", d) for d in (1, 2, 3)]
        terms = [b[:, None, None] * v[None] for b, v in zip(basis, parts)]
        line = (terms[0] + terms[1]) + (terms[2] + terms[3])
        return line + swap(line, "freq", 4)

    def project(poly):
        return jnp.sum(basis[0][:, None, None] * poly, axis=0)

    ids = stations[0].reshape(-1)
    pick = (ids[None, :] == jnp.arange(S, dtype=jnp.int32)[:, None]).astype(bf16)
    pick = jnp.concatenate([pick, pick], axis=0)
    place = (ids[:, None] == jnp.arange(S, dtype=jnp.int32)[None, :]).astype(bf16)
    place = jnp.concatenate([place, place], axis=0)
    slot = np.arange(K)
    mask = ((slot & 3) * 4 + (slot >> 2 & 3)) * 2 + (slot >> 4 & 1)
    source = 2 * (tm ^ jnp.asarray(mask, jnp.int32)) + jnp.asarray(slot >> 5, jnp.int32)
    order = (source[:, None] == jnp.arange(K, dtype=jnp.int32)[None, :]).astype(bf16)
    sky = jnp.einsum("ak,ckn->can", order, coherency[0, 0], preferred_element_type=f32).reshape(8 * K, -1)

    own, other = spread_over_tm(start)
    fitted = project(consensus_of(start + dual_now / rho))
    gown, gother = gradient(weight, own, other, sky, pick, place, visibilities[0, 0])
    descent = sum_over_tm(gown, gother) + dual_now + rho * (start - fitted)
    down, dother = spread_over_tm(descent)
    gown, gother, rate = gradient(weight, own, other, sky, pick, place, visibilities[0, 0], (down, dother))
    current = start - rate[0, 0] * descent
    fitted = project(consensus_of(current + dual_now / rho))
    dual_now = dual_now + rho * (current - fitted)

    descent = sum_over_tm(gown, gother) + dual_now + rho * (current - fitted)
    squares = jnp.broadcast_to(jnp.sum(descent * descent), (32, 1, 128))
    squares = jnp.sum(lax.all_to_all(squares, "tm", 0, 0, tiled=True)[:, 0, 0])
    current = current - step_size * descent / jnp.sqrt(squares / (8.0 * K * S) + epsilon)
    poly = consensus_of(current + dual_now / rho)
    dual_now = dual_now + rho * (current - project(poly))
    return unpacked(current), unpacked(dual_now), unpacked(poly)


def solution(mesh):
    return jax.shard_map(
        body,
        mesh=mesh,
        in_specs=(
            P("tm", "freq", None, None),
            P("tm", "freq", None, None, None),
            P("tm", None, None),
            P("freq", None, "tm"),
            P("freq", None, "tm"),
            P(),
            P(),
        ),
        out_specs=(P("freq", None, "tm"), P("freq", None, "tm"), P(None, None, "tm")),
        check_vma=False,
    )
```

```python
import functools
import math

import jax
import jax.numpy as jnp
import numpy as np
from jax import lax
from jax.experimental import pallas as pl
from jax.experimental.pallas import tpu as pltpu
from jax.sharding import Mesh
from jax.sharding import PartitionSpec as P

S = 512
K = 64
step_size = 0.5
epsilon = 1e-06


f32 = jnp.float32
bf16 = jnp.bfloat16


def poly_basis(channels, degrees):
    points = np.linspace(-1.0, 1.0, channels)
    columns = []
    for degree in range(degrees):
        column = points**degree
        for earlier in columns:
            column = column - np.dot(earlier, column) * earlier
        column = column / np.sqrt(np.dot(column, column))
        columns.append(column)
    return np.stack(columns, axis=1).astype(np.float32)


def swap(value, axis, mask):
    size = {"tm": 32, "zh": 2, "y": 4}[axis]
    return lax.ppermute(value, axis, [(i, i ^ mask) for i in range(size)])


def spread(value):
    own = jnp.concatenate([value] + [swap(value, "tm", 8 * d) for d in (1, 2, 3)], axis=0)
    return own, swap(own, "tm", 1)


def collect(own, other):
    line = (own + swap(other, "tm", 1)).reshape(4, 64, 128)
    parts = [line[0]] + [swap(line[d], "tm", 8 * d) for d in (1, 2, 3)]
    return (parts[0] + parts[1]) + (parts[2] + parts[3])


def pair_times(a, b):
    return (a[0] * b[0] - a[1] * b[1], a[0] * b[1] + a[1] * b[0])


def pair_times_conj(a, b):
    return (a[0] * b[0] + a[1] * b[1], a[1] * b[0] - a[0] * b[1])


def pair_conj_times(a, b):
    return (a[0] * b[0] + a[1] * b[1], a[0] * b[1] - a[1] * b[0])


def pair_add(a, b):
    return (a[0] + b[0], a[1] + b[1])


def matrix(parts):
    return [[(parts[0], parts[1]), (parts[2], parts[3])], [(parts[4], parts[5]), (parts[6], parts[7])]]


def flat(m):
    return [m[0][0][0], m[0][0][1], m[0][1][0], m[0][1][1], m[1][0][0], m[1][0][1], m[1][1][0], m[1][1][1]]


def times(a, b):
    return [[pair_add(pair_times(a[i][0], b[0][j]), pair_times(a[i][1], b[1][j])) for j in range(2)] for i in range(2)]


def times_h(a, b):
    return [
        [pair_add(pair_times_conj(a[i][0], b[j][0]), pair_times_conj(a[i][1], b[j][1])) for j in range(2)]
        for i in range(2)
    ]


def h_times(a, b):
    return [
        [pair_add(pair_conj_times(a[0][i], b[0][j]), pair_conj_times(a[1][i], b[1][j])) for j in range(2)]
        for i in range(2)
    ]


def split(value):
    high = value.astype(bf16)
    return high, (value - high.astype(f32)).astype(bf16)


VMEM = pl.BlockSpec(memory_space=pltpu.VMEM)


def call(body, outs, scratch, args, aliases=None, smem=0):
    return pl.pallas_call(
        body,
        out_shape=[jax.ShapeDtypeStruct(*o) for o in outs],
        in_specs=[pl.BlockSpec(memory_space=pltpu.SMEM)] * smem + [VMEM] * (len(args) - smem),
        out_specs=[VMEM] * len(outs),
        scratch_shapes=[pltpu.VMEM(*b) for b in scratch],
        compiler_params=pltpu.CompilerParams(vmem_limit_bytes=28 << 20),
        input_output_aliases=aliases or {},
    )(*args)


def last_kernel(degrees, near0, near1, near2, near3, basis, current, dual, rho, out, dual_out, poly):
    fitted = None
    for j in range(degrees):
        sums = []
        for half in range(2):
            rows = slice(half * 64, half * 64 + 64)
            terms = [
                basis[half * 4 + d : half * 4 + d + 1, j : j + 1] * ref[rows, :]
                for d, ref in enumerate((near0, near1, near2, near3))
            ]
            sums.append((terms[0] + terms[1]) + (terms[2] + terms[3]))
        coefficient = sums[0] + sums[1]
        poly[j * 64 : j * 64 + 64, :] = coefficient
        term = basis[0:1, j : j + 1] * coefficient
        fitted = term if fitted is None else fitted + term
    out[...] = current[...]
    dual_out[...] = dual[...] + rho[...] * (current[...] - fitted)


def step_kernel(count, zh, squares, value, down, far_value, far_down, current, pair, out):
    owner = lax.broadcasted_iota(jnp.int32, (64, 128), 0) & 1
    steps = []
    for side in (zh[0], 1 - zh[0]):
        kept = jnp.where(owner == side, squares[...], 0.0)
        total = jnp.sum(jnp.sum(kept, axis=0, keepdims=True), axis=1, keepdims=True)
        steps.append(step_size / jnp.sqrt(total / count + epsilon))
    pair[0:64, :] = value[...] - steps[0] * down[...]
    pair[64:128, :] = far_value[...] - steps[1] * far_down[...]
    out[...] = current[...] - steps[0] * down[...]


def stations_of(sky):
    rows = sky[128:144, :].astype(f32)
    return [rows[2 * side : 2 * side + 1] * 16.0 + rows[2 * side + 1 : 2 * side + 2] for side in range(2)]


def place_table_kernel(sky0, sky1, sky2, sky3, after, out):
    station = lax.broadcasted_iota(jnp.int32, (512, 512), 1).astype(f32)
    rows = [row for sky in (sky0, sky1, sky2, sky3) for row in stations_of(sky)]
    columns = jnp.concatenate(rows, axis=0).T
    for j in range(8):
        hit = station == columns[:, j : j + 1]
        out[j * 512 : j * 512 + 512, :] = jnp.where(hit, 1.0, 0.0).astype(bf16)


def sky_kernel(tm, coherency, stations, *outs):
    slot = lax.broadcasted_iota(jnp.int32, (64, 64), 0)
    owner = tm[0] ^ ((slot & 3) * 8 + (slot >> 4) * 2 + ((slot >> 2) & 1))
    order = owner * 2 + ((slot >> 3) & 1) == lax.broadcasted_iota(jnp.int32, (64, 64), 1)
    order = jnp.where(order, 1.0, 0.0).astype(bf16)
    for c in range(8):
        rows = jnp.dot(order, coherency[c], preferred_element_type=f32).astype(bf16)
        for d in range(4):
            outs[d][c * 16 : c * 16 + 16, :] = rows[d * 16 : d * 16 + 16, :]
    ids = stations[...]
    parts = [part for side in range(2) for part in (ids[side : side + 1] >> 4, ids[side : side + 1] & 15)]
    rows = jnp.concatenate(parts + [jnp.zeros((12, 512), jnp.int32)], axis=0).astype(f32).astype(bf16)
    for d in range(4):
        outs[d][128:144, :] = rows


def pick_kernel(own, other, sky0, sky1, sky2, sky3, gains, stage, lhs, table):
    stage[0:256, :] = own[...]
    stage[256:512, :] = other[...]
    for c in range(8):
        for block in range(4):
            first = stage[pl.ds(block * 8 + c, 8, stride=64), :]
            second = stage[pl.ds(block * 8 + 32 + c, 8, stride=64), :]
            high, low = split(jnp.concatenate([first, second], axis=0))
            lanes = slice(block * 128, block * 128 + 128)
            lhs[c * 16 : c * 16 + 16, lanes] = high
            lhs[128 + c * 16 : 144 + c * 16, lanes] = low
    station = lax.broadcasted_iota(jnp.int32, (512, 512), 0).astype(f32)
    for s, sky in enumerate((sky0, sky1, sky2, sky3)):
        for side, row in enumerate(stations_of(sky)):
            hit = station == row
            table[s % 2, :, side * 512 : side * 512 + 512] = jnp.where(hit, 1.0, 0.0).astype(bf16)
        both = jnp.dot(lhs[...], table[s % 2], preferred_element_type=f32)
        gains[:, s * 1024 : s * 1024 + 1024] = both[0:128] + both[128:256]


def halves(ref, c, lanes):
    rows = ref[c * 16 : c * 16 + 16, lanes].astype(f32)
    return rows[0:8], rows[8:16]


def model_kernel(count, moved, *refs):
    if moved:
        before, delta, n0, n1, n2, n3, sky0, sky1, sky2, sky3, vis, gains, part, rate = refs
        total = (n0[...] + n1[...]) + (n2[...] + n3[...])
        mean = jnp.sum(total, axis=(0, 1), keepdims=True) / count
        step = jnp.broadcast_to(step_size / jnp.sqrt(mean + epsilon), (8, 128))
        rate[...] = step
    else:
        gains, sky0, sky1, sky2, sky3, vis, part = refs
    for s, sky in enumerate((sky0, sky1, sky2, sky3)):

        def block(nb, carry, s=s, sky=sky):
            def at(base):
                return pl.ds(pl.multiple_of(base + nb * 128, 128), 128)

            here, plane, qlane = at(0), at(s * 1024), at(s * 1024 + 512)
            models = [halves(sky, c, here) for c in range(8)]
            sums = None
            for h in range(2):
                ends = []
                for lanes in (plane, qlane):
                    values = []
                    for c in range(8):
                        rows = slice(c * 16 + h * 8, c * 16 + h * 8 + 8)
                        if moved:
                            value = before[rows, lanes] - step * delta[rows, lanes]
                            gains[rows, lanes] = value
                        else:
                            value = gains[rows, lanes]
                        values.append(value)
                    ends.append(matrix(values))
                product = times(ends[0], matrix([m[h] for m in models]))
                result = flat(times_h(product, ends[1]))
                sums = result if sums is None else [a + b for a, b in zip(sums, result)]
            for c in range(8):
                row = jnp.sum(sums[c], axis=0, keepdims=True)
                if s == 0:
                    row = row - vis[c : c + 1, here]
                part[s * 8 + c : s * 8 + c + 1, here] = row
            return carry

        lax.fori_loop(0, 4, block, 0)


def terms_kernel(weight, part, r1, r2, r3, gains, sky0, sky1, sky2, sky3, place, gown, gother, terms, stage):
    for s, sky in enumerate((sky0, sky1, sky2, sky3)):

        def block(nb, carry, s=s, sky=sky):
            def at(base):
                return pl.ds(pl.multiple_of(base + nb * 128, 128), 128)

            def slot(ref, t):
                return ref[t * 8 : t * 8 + 8, at(0)]

            error = (slot(part, s) + slot(r1, s ^ 1)) + (slot(r2, s ^ 2) + slot(r3, s ^ 3))
            error = error * weight
            errors = matrix([jnp.broadcast_to(error[c : c + 1], (8, 128)) for c in range(8)])
            models = [halves(sky, c, at(0)) for c in range(8)]
            outs = ([], [])
            for h in range(2):
                rows = [slice(c * 16 + h * 8, c * 16 + h * 8 + 8) for c in range(8)]
                model = matrix([m[h] for m in models])
                second = matrix([gains[r, at(s * 1024 + 512)] for r in rows])
                outs[0].append(flat(times(errors, times_h(second, model))))
                first = matrix([gains[r, at(s * 1024)] for r in rows])
                outs[1].append(flat(h_times(errors, times(first, model))))
            for side in range(2):
                lanes = at(s * 1024 + side * 512)
                for c in range(8):
                    high, low = split(jnp.concatenate([outs[side][0][c], outs[side][1][c]], axis=0))
                    terms[c * 16 : c * 16 + 16, lanes] = high
                    terms[128 + c * 16 : 144 + c * 16, lanes] = low
            return carry

        lax.fori_loop(0, 4, block, 0)
    both = jnp.dot(terms[...], place[...], preferred_element_type=f32)
    sums = both[0:128] + both[128:256]
    for c in range(8):
        for block in range(8):
            row = c * 16 + block // 4 * 8
            lane = block % 4 * 128
            stage[pl.ds(block * 8 + c, 8, stride=64), :] = sums[row : row + 8, lane : lane + 128]
    gown[...] = stage[0:256, :]
    gother[...] = stage[256:512, :]


def body(visibilities, coherency, stations, jones, dual, cluster, rho_table):
    channels = lax.axis_size("zh") * lax.axis_size("y")
    degrees = min(3, channels - 1)
    tm = lax.axis_index("tm")
    zh = lax.axis_index("zh")
    freq = zh * 4 + lax.axis_index("y")
    weight = np.float32(math.sqrt(S / (2.0 * lax.axis_size("tm") * visibilities.shape[3])))
    count = 8.0 * K * S

    def packed(value):
        return value.reshape(8, 8, 128).transpose(1, 0, 2).reshape(64, 128)

    def unpacked(value):
        return value.reshape(-1, 8, 8, 128).transpose(0, 2, 1, 3).reshape(-1, 8, 1024)

    start = packed(jones[0])
    dual_start = packed(dual[0])
    rho_dir = jnp.sum(
        jnp.where(cluster[:, None] == jnp.arange(rho_table.shape[0], dtype=jnp.int32)[None, :], rho_table[None, :], 0.0),
        axis=1,
    )
    rho = jnp.repeat(lax.dynamic_slice_in_dim(rho_dir, tm * 2, 2), 32)[:, None]
    table = jnp.asarray(poly_basis(channels, degrees))
    basis = [lax.dynamic_index_in_dim(table, freq ^ d, 0, keepdims=False) for d in range(8)]

    def y_line(value):
        return [value] + [swap(value, "y", d) for d in (1, 2, 3)]

    def consensus_of(value):
        pair = jnp.stack([value, swap(value, "zh", 1)])
        parts = y_line(pair)
        sums = []
        for half in range(2):
            rows = basis[half * 4 : half * 4 + 4]
            terms = [b.reshape((-1,) + (1,) * value.ndim) * v[half][None] for b, v in zip(rows, parts)]
            sums.append((terms[0] + terms[1]) + (terms[2] + terms[3]))
        return sums[0] + sums[1]

    def project(poly):
        return jnp.sum(basis[0][:, None, None] * poly, axis=0)

    own, other = spread(start)
    args = (tm.astype(jnp.int32).reshape(1), coherency[0, 0], stations[0])
    skies = call(sky_kernel, [((144, 512), bf16)] * 4, [], args, smem=1)
    skies = [skies[0]] + [swap(skies[d], "tm", 2 * d) for d in (1, 2, 3)]
    vis = visibilities[0, 0]
    many = ((128, 4096), f32)
    model_outs = [((32, 512), f32)]

    def gains_of(own, other):
        scratch = [((512, 128), f32), ((256, 512), bf16), ((2, 512, 1024), bf16)]
        return call(pick_kernel, [many], scratch, (own, other, *skies))[0]

    def gradient_of(gains, part):
        others = [swap(part, "tm", 2 * d) for d in (1, 2, 3)]
        outs = [((256, 128), f32)] * 2
        scratch = [((256, 4096), bf16), ((512, 128), f32)]
        place = call(place_table_kernel, [((4096, 512), bf16)], [], (*skies, part))[0]
        args = (part, *others, gains, *skies, place)
        return collect(*call(functools.partial(terms_kernel, weight), outs, scratch, args))

    gains = gains_of(own, other)
    (part,) = call(functools.partial(model_kernel, count, False), model_outs, [], (gains, *skies, vis))

    fitted = project(consensus_of(start + dual_start / rho))
    descent = gradient_of(gains, part) + dual_start + rho * (start - fitted)

    down, dother = spread(descent)
    norm = jnp.sum((down * down + dother * dother).reshape(32, 8, 128), axis=0)
    norms = [norm] + [swap(norm, "tm", 2 * d) for d in (1, 2, 3)]
    delta = gains_of(down, dother)
    gains, part, rate = call(
        functools.partial(model_kernel, count, True),
        [many] + model_outs + [((8, 128), f32)],
        [],
        (gains, delta, *norms, *skies, vis),
        {0: 0},
    )
    current = start - rate[0:1, :] * descent
    fitted = project(consensus_of(current + dual_start / rho))
    dual_now = dual_start + rho * (current - fitted)

    descent = gradient_of(gains, part) + dual_now + rho * (current - fitted)
    near = jnp.stack([current + dual_now / rho, descent])
    far = swap(near, "zh", 1)
    squares = jnp.sum((descent * descent).reshape(64, 128), axis=0)[None, None, :]
    squares = lax.all_to_all(jnp.broadcast_to(squares, (64, 1, 128)), ("tm", "zh"), 0, 0, tiled=True).reshape(64, 128)
    args = (zh.astype(jnp.int32).reshape(1), squares, near[0], near[1], far[0], far[1], current)
    outs = [((128, 128), f32), ((64, 128), f32)]
    pair, current = call(functools.partial(step_kernel, count), outs, [], args, smem=1)
    lines = y_line(pair)
    rows = jnp.zeros((8, 128), f32).at[:, :degrees].set(jnp.stack(basis))
    args = (*lines, rows, current, dual_now, jnp.broadcast_to(rho, (64, 128)))
    outs = [((64, 128), f32), ((64, 128), f32), ((degrees * 64, 128), f32)]
    current, dual_now, poly = call(functools.partial(last_kernel, degrees), outs, [], args)
    return unpacked(current), unpacked(dual_now), unpacked(poly)


def solution(mesh):
    fine = Mesh(mesh.devices.reshape(32, 2, 4), ("tm", "zh", "y"))
    freq = ("zh", "y")

    return jax.shard_map(
        body,
        mesh=fine,
        in_specs=(
            P("tm", freq, None, None),
            P("tm", freq, None, None, None),
            P("tm", None, None),
            P(freq, None, "tm"),
            P(freq, None, "tm"),
            P(),
            P(),
        ),
        out_specs=(P(freq, None, "tm"), P(freq, None, "tm"), P(None, None, "tm")),
        check_vma=False,
    )
```

```python
import functools
import math

import jax
import jax.numpy as jnp
import numpy as np
from jax import lax
from jax.experimental import pallas as pl
from jax.experimental.pallas import tpu as pltpu
from jax.sharding import Mesh
from jax.sharding import PartitionSpec as P

S = 512
K = 64
step_size = 0.5
epsilon = 1e-06


f32 = jnp.float32
bf16 = jnp.bfloat16


def poly_basis(channels, degrees):
    points = np.linspace(-1.0, 1.0, channels)
    columns = []
    for degree in range(degrees):
        column = points**degree
        for earlier in columns:
            column = column - np.dot(earlier, column) * earlier
        column = column / np.sqrt(np.dot(column, column))
        columns.append(column)
    return np.stack(columns, axis=1).astype(np.float32)


def swap(value, axis, mask):
    size = {"tm": 32, "zh": 2, "y": 4}[axis]
    return lax.ppermute(value, axis, [(i, i ^ mask) for i in range(size)])


def spread(value):
    own = jnp.concatenate([value] + [swap(value, "tm", 8 * d) for d in (1, 2, 3)], axis=0)
    return own, swap(own, "tm", 1)


def collect(own, other):
    line = (own + swap(other, "tm", 1)).reshape(4, 64, 128)
    parts = [line[0]] + [swap(line[d], "tm", 8 * d) for d in (1, 2, 3)]
    return (parts[0] + parts[1]) + (parts[2] + parts[3])


def pair_times(a, b):
    return (a[0] * b[0] - a[1] * b[1], a[0] * b[1] + a[1] * b[0])


def pair_times_conj(a, b):
    return (a[0] * b[0] + a[1] * b[1], a[1] * b[0] - a[0] * b[1])


def pair_conj_times(a, b):
    return (a[0] * b[0] + a[1] * b[1], a[0] * b[1] - a[1] * b[0])


def pair_add(a, b):
    return (a[0] + b[0], a[1] + b[1])


def matrix(parts):
    return [[(parts[0], parts[1]), (parts[2], parts[3])], [(parts[4], parts[5]), (parts[6], parts[7])]]


def flat(m):
    return [m[0][0][0], m[0][0][1], m[0][1][0], m[0][1][1], m[1][0][0], m[1][0][1], m[1][1][0], m[1][1][1]]


def times(a, b):
    return [[pair_add(pair_times(a[i][0], b[0][j]), pair_times(a[i][1], b[1][j])) for j in range(2)] for i in range(2)]


def times_h(a, b):
    return [
        [pair_add(pair_times_conj(a[i][0], b[j][0]), pair_times_conj(a[i][1], b[j][1])) for j in range(2)]
        for i in range(2)
    ]


def h_times(a, b):
    return [
        [pair_add(pair_conj_times(a[0][i], b[0][j]), pair_conj_times(a[1][i], b[1][j])) for j in range(2)]
        for i in range(2)
    ]


def split(value):
    high = value.astype(bf16)
    return high, (value - high.astype(f32)).astype(bf16)


VMEM = pl.BlockSpec(memory_space=pltpu.VMEM)


def call(body, outs, scratch, args, aliases=None, smem=0):
    return pl.pallas_call(
        body,
        out_shape=[jax.ShapeDtypeStruct(*o) for o in outs],
        in_specs=[pl.BlockSpec(memory_space=pltpu.SMEM)] * smem + [VMEM] * (len(args) - smem),
        out_specs=[VMEM] * len(outs),
        scratch_shapes=[pltpu.VMEM(*b) for b in scratch],
        compiler_params=pltpu.CompilerParams(vmem_limit_bytes=28 << 20),
        input_output_aliases=aliases or {},
    )(*args)


def last_kernel(degrees, near0, near1, near2, near3, basis, current, dual, rho, out, dual_out, poly):
    fitted = None
    for j in range(degrees):
        sums = []
        for half in range(2):
            rows = slice(half * 64, half * 64 + 64)
            terms = [
                basis[half * 4 + d : half * 4 + d + 1, j : j + 1] * ref[rows, :]
                for d, ref in enumerate((near0, near1, near2, near3))
            ]
            sums.append((terms[0] + terms[1]) + (terms[2] + terms[3]))
        coefficient = sums[0] + sums[1]
        poly[j * 64 : j * 64 + 64, :] = coefficient
        term = basis[0:1, j : j + 1] * coefficient
        fitted = term if fitted is None else fitted + term
    out[...] = current[...]
    dual_out[...] = dual[...] + rho[...] * (current[...] - fitted)


def step_kernel(count, zh, squares, value, down, far_value, far_down, current, pair, out):
    owner = lax.broadcasted_iota(jnp.int32, (64, 128), 0) & 1
    steps = []
    for side in (zh[0], 1 - zh[0]):
        kept = jnp.where(owner == side, squares[...], 0.0)
        total = jnp.sum(jnp.sum(kept, axis=0, keepdims=True), axis=1, keepdims=True)
        steps.append(step_size / jnp.sqrt(total / count + epsilon))
    pair[0:64, :] = value[...] - steps[0] * down[...]
    pair[64:128, :] = far_value[...] - steps[1] * far_down[...]
    out[...] = current[...] - steps[0] * down[...]


def stations_of(sky):
    rows = sky[128:144, :].astype(f32)
    return [rows[2 * side : 2 * side + 1] * 16.0 + rows[2 * side + 1 : 2 * side + 2] for side in range(2)]


def place_table_kernel(sky0, sky1, sky2, sky3, after, out):
    station = lax.broadcasted_iota(jnp.int32, (512, 512), 1).astype(f32)
    rows = [row for sky in (sky0, sky1, sky2, sky3) for row in stations_of(sky)]
    columns = jnp.concatenate(rows, axis=0).T
    for j in range(8):
        hit = station == columns[:, j : j + 1]
        out[j * 512 : j * 512 + 512, :] = jnp.where(hit, 1.0, 0.0).astype(bf16)


def sky_kernel(tm, coherency, stations, *outs):
    slot = lax.broadcasted_iota(jnp.int32, (64, 64), 0)
    owner = tm[0] ^ ((slot & 3) * 8 + (slot >> 4) * 2 + ((slot >> 2) & 1))
    order = owner * 2 + ((slot >> 3) & 1) == lax.broadcasted_iota(jnp.int32, (64, 64), 1)
    order = jnp.where(order, 1.0, 0.0).astype(bf16)
    for c in range(8):
        rows = jnp.dot(order, coherency[c], preferred_element_type=f32).astype(bf16)
        for d in range(4):
            outs[d][c * 16 : c * 16 + 16, :] = rows[d * 16 : d * 16 + 16, :]
    ids = stations[...]
    parts = [part for side in range(2) for part in (ids[side : side + 1] >> 4, ids[side : side + 1] & 15)]
    rows = jnp.concatenate(parts + [jnp.zeros((12, 512), jnp.int32)], axis=0).astype(f32).astype(bf16)
    for d in range(4):
        outs[d][128:144, :] = rows


def pick_kernel(own, other, sky0, sky1, sky2, sky3, gains, stage, lhs, table):
    stage[0:256, :] = own[...]
    stage[256:512, :] = other[...]
    for c in range(8):
        for block in range(4):
            first = stage[pl.ds(block * 8 + c, 8, stride=64), :]
            second = stage[pl.ds(block * 8 + 32 + c, 8, stride=64), :]
            high, low = split(jnp.concatenate([first, second], axis=0))
            lanes = slice(block * 128, block * 128 + 128)
            lhs[c * 16 : c * 16 + 16, lanes] = high
            lhs[128 + c * 16 : 144 + c * 16, lanes] = low
    station = lax.broadcasted_iota(jnp.int32, (512, 512), 0).astype(f32)
    for s, sky in enumerate((sky0, sky1, sky2, sky3)):
        for side, row in enumerate(stations_of(sky)):
            hit = station == row
            table[s % 2, :, side * 512 : side * 512 + 512] = jnp.where(hit, 1.0, 0.0).astype(bf16)
        both = jnp.dot(lhs[...], table[s % 2], preferred_element_type=f32)
        gains[:, s * 1024 : s * 1024 + 1024] = both[0:128] + both[128:256]


def halves(ref, c, lanes):
    rows = ref[c * 16 : c * 16 + 16, lanes].astype(f32)
    return rows[0:8], rows[8:16]


def model_kernel(count, moved, *refs):
    if moved:
        before, delta, n0, n1, n2, n3, sky0, sky1, sky2, sky3, vis, gains, part, rate = refs
        total = (n0[...] + n1[...]) + (n2[...] + n3[...])
        mean = jnp.sum(total, axis=(0, 1), keepdims=True) / count
        step = jnp.broadcast_to(step_size / jnp.sqrt(mean + epsilon), (8, 128))
        rate[...] = step
    else:
        gains, sky0, sky1, sky2, sky3, vis, part = refs
    for s, sky in enumerate((sky0, sky1, sky2, sky3)):

        def block(nb, carry, s=s, sky=sky):
            def at(base):
                return pl.ds(pl.multiple_of(base + nb * 128, 128), 128)

            here, plane, qlane = at(0), at(s * 1024), at(s * 1024 + 512)
            models = [halves(sky, c, here) for c in range(8)]
            sums = None
            for h in range(2):
                ends = []
                for lanes in (plane, qlane):
                    values = []
                    for c in range(8):
                        rows = slice(c * 16 + h * 8, c * 16 + h * 8 + 8)
                        if moved:
                            value = before[rows, lanes] - step * delta[rows, lanes]
                            gains[rows, lanes] = value
                        else:
                            value = gains[rows, lanes]
                        values.append(value)
                    ends.append(matrix(values))
                product = times(ends[0], matrix([m[h] for m in models]))
                result = flat(times_h(product, ends[1]))
                sums = result if sums is None else [a + b for a, b in zip(sums, result)]
            for c in range(8):
                row = jnp.sum(sums[c], axis=0, keepdims=True)
                if s == 0:
                    row = row - vis[c : c + 1, here]
                part[s * 8 + c : s * 8 + c + 1, here] = row
            return carry

        lax.fori_loop(0, 4, block, 0)


def terms_kernel(weight, part, r1, r2, r3, gains, sky0, sky1, sky2, sky3, place, gown, gother, terms, stage):
    for s, sky in enumerate((sky0, sky1, sky2, sky3)):

        def block(nb, carry, s=s, sky=sky):
            def at(base):
                return pl.ds(pl.multiple_of(base + nb * 128, 128), 128)

            def slot(ref, t):
                return ref[t * 8 : t * 8 + 8, at(0)]

            error = (slot(part, s) + slot(r1, s ^ 1)) + (slot(r2, s ^ 2) + slot(r3, s ^ 3))
            error = error * weight
            errors = matrix([jnp.broadcast_to(error[c : c + 1], (8, 128)) for c in range(8)])
            models = [halves(sky, c, at(0)) for c in range(8)]
            outs = ([], [])
            for h in range(2):
                rows = [slice(c * 16 + h * 8, c * 16 + h * 8 + 8) for c in range(8)]
                model = matrix([m[h] for m in models])
                second = matrix([gains[r, at(s * 1024 + 512)] for r in rows])
                outs[0].append(flat(times(errors, times_h(second, model))))
                first = matrix([gains[r, at(s * 1024)] for r in rows])
                outs[1].append(flat(h_times(errors, times(first, model))))
            for side in range(2):
                lanes = at(s * 1024 + side * 512)
                for c in range(8):
                    high, low = split(jnp.concatenate([outs[side][0][c], outs[side][1][c]], axis=0))
                    terms[c * 16 : c * 16 + 16, lanes] = high
                    terms[128 + c * 16 : 144 + c * 16, lanes] = low
            return carry

        lax.fori_loop(0, 4, block, 0)
    both = jnp.dot(terms[...], place[...], preferred_element_type=f32)
    sums = both[0:128] + both[128:256]
    for c in range(8):
        for block in range(8):
            row = c * 16 + block // 4 * 8
            lane = block % 4 * 128
            stage[pl.ds(block * 8 + c, 8, stride=64), :] = sums[row : row + 8, lane : lane + 128]
    gown[...] = stage[0:256, :]
    gother[...] = stage[256:512, :]


def body(visibilities, coherency, stations, jones, dual, cluster, rho_table):
    channels = lax.axis_size("zh") * lax.axis_size("y")
    degrees = min(3, channels - 1)
    tm = lax.axis_index("tm")
    zh = lax.axis_index("zh")
    freq = zh * 4 + lax.axis_index("y")
    weight = np.float32(math.sqrt(S / (2.0 * lax.axis_size("tm") * visibilities.shape[3])))
    count = 8.0 * K * S

    def packed(value):
        return value.reshape(8, 8, 128).transpose(1, 0, 2).reshape(64, 128)

    def unpacked(value):
        return value.reshape(-1, 8, 8, 128).transpose(0, 2, 1, 3).reshape(-1, 8, 1024)

    start = packed(jones[0])
    dual_start = packed(dual[0])
    rho_dir = jnp.sum(
        jnp.where(cluster[:, None] == jnp.arange(rho_table.shape[0], dtype=jnp.int32)[None, :], rho_table[None, :], 0.0),
        axis=1,
    )
    rho = jnp.repeat(lax.dynamic_slice_in_dim(rho_dir, tm * 2, 2), 32)[:, None]
    table = poly_basis(channels, degrees)
    wide = np.zeros((channels, 8, 128), np.float32)
    for f in range(channels):
        wide[f, :, :degrees] = [table[f ^ d] for d in range(8)]
    rows = lax.dynamic_index_in_dim(jnp.asarray(wide), freq, 0, keepdims=False)
    basis = [rows[d, :degrees] for d in range(8)]

    def y_line(value):
        return [value] + [swap(value, "y", d) for d in (1, 2, 3)]

    def consensus_of(value):
        pair = jnp.stack([value, swap(value, "zh", 1)])
        parts = y_line(pair)
        sums = []
        for half in range(2):
            rows = basis[half * 4 : half * 4 + 4]
            terms = [b.reshape((-1,) + (1,) * value.ndim) * v[half][None] for b, v in zip(rows, parts)]
            sums.append((terms[0] + terms[1]) + (terms[2] + terms[3]))
        return sums[0] + sums[1]

    def project(poly):
        return jnp.sum(basis[0][:, None, None] * poly, axis=0)

    own, other = spread(start)
    args = (tm.astype(jnp.int32).reshape(1), coherency[0, 0], stations[0])
    skies = call(sky_kernel, [((144, 512), bf16)] * 4, [], args, smem=1)
    skies = [skies[0]] + [swap(skies[d], "tm", 2 * d) for d in (1, 2, 3)]
    vis = visibilities[0, 0]
    many = ((128, 4096), f32)
    model_outs = [((32, 512), f32)]

    def gains_of(own, other):
        scratch = [((512, 128), f32), ((256, 512), bf16), ((2, 512, 1024), bf16)]
        return call(pick_kernel, [many], scratch, (own, other, *skies))[0]

    def gradient_of(gains, part):
        others = [swap(part, "tm", 2 * d) for d in (1, 2, 3)]
        outs = [((256, 128), f32)] * 2
        scratch = [((256, 4096), bf16), ((512, 128), f32)]
        place = call(place_table_kernel, [((4096, 512), bf16)], [], (*skies, part))[0]
        args = (part, *others, gains, *skies, place)
        return collect(*call(functools.partial(terms_kernel, weight), outs, scratch, args))

    gains = gains_of(own, other)
    (part,) = call(functools.partial(model_kernel, count, False), model_outs, [], (gains, *skies, vis))

    fitted = project(consensus_of(start + dual_start / rho))
    descent = gradient_of(gains, part) + dual_start + rho * (start - fitted)

    down, dother = spread(descent)
    norm = jnp.sum((down * down + dother * dother).reshape(32, 8, 128), axis=0)
    norms = [norm] + [swap(norm, "tm", 2 * d) for d in (1, 2, 3)]
    delta = gains_of(down, dother)
    gains, part, rate = call(
        functools.partial(model_kernel, count, True),
        [many] + model_outs + [((8, 128), f32)],
        [],
        (gains, delta, *norms, *skies, vis),
        {0: 0},
    )
    current = start - rate[0:1, :] * descent
    fitted = project(consensus_of(current + dual_start / rho))
    dual_now = dual_start + rho * (current - fitted)

    descent = gradient_of(gains, part) + dual_now + rho * (current - fitted)
    near = jnp.stack([current + dual_now / rho, descent])
    far = swap(near, "zh", 1)
    squares = jnp.broadcast_to(jnp.sum(descent * descent, axis=0, keepdims=True), (64, 128))
    squares = lax.optimization_barrier(squares).reshape(64, 1, 128)
    squares = lax.all_to_all(squares, ("tm", "zh"), 0, 0, tiled=True).reshape(64, 128)
    args = (zh.astype(jnp.int32).reshape(1), squares, near[0], near[1], far[0], far[1], current)
    outs = [((128, 128), f32), ((64, 128), f32)]
    pair, current = call(functools.partial(step_kernel, count), outs, [], args, smem=1)
    lines = y_line(pair)
    args = (*lines, rows, current, dual_now, jnp.broadcast_to(rho, (64, 128)))
    outs = [((64, 128), f32), ((64, 128), f32), ((degrees * 64, 128), f32)]
    current, dual_now, poly = call(functools.partial(last_kernel, degrees), outs, [], args)
    return unpacked(current), unpacked(dual_now), unpacked(poly)


def solution(mesh):
    fine = Mesh(mesh.devices.reshape(32, 2, 4), ("tm", "zh", "y"))
    freq = ("zh", "y")

    return jax.shard_map(
        body,
        mesh=fine,
        in_specs=(
            P("tm", freq, None, None),
            P("tm", freq, None, None, None),
            P("tm", None, None),
            P(freq, None, "tm"),
            P(freq, None, "tm"),
            P(),
            P(),
        ),
        out_specs=(P(freq, None, "tm"), P(freq, None, "tm"), P(None, None, "tm")),
        check_vma=False,
    )
```

```python
import functools
import math

import jax
import jax.numpy as jnp
import numpy as np
from jax import lax
from jax.experimental import pallas as pl
from jax.experimental.pallas import tpu as pltpu
from jax.sharding import Mesh
from jax.sharding import PartitionSpec as P

S = 512
K = 64
step_size = 0.5
epsilon = 1e-06


f32 = jnp.float32
bf16 = jnp.bfloat16


def poly_basis(channels, degrees):
    points = np.linspace(-1.0, 1.0, channels)
    columns = []
    for degree in range(degrees):
        column = points**degree
        for earlier in columns:
            column = column - np.dot(earlier, column) * earlier
        column = column / np.sqrt(np.dot(column, column))
        columns.append(column)
    return np.stack(columns, axis=1).astype(np.float32)


def swap(value, axis, mask):
    size = {"tm": 32, "zh": 2, "y": 4}[axis]
    return lax.ppermute(value, axis, [(i, i ^ mask) for i in range(size)])


def spread(value):
    parts = [value] + [swap(value, "tm", 8 * d) for d in (1, 2, 3)]
    own = call(join_kernel, [((256, 128), f32)], [], parts)[0]
    return own, swap(own, "tm", 1)


def collect(own, other):
    line = (own + swap(other, "tm", 1)).reshape(4, 64, 128)
    parts = [line[0]] + [swap(line[d], "tm", 8 * d) for d in (1, 2, 3)]
    return (parts[0] + parts[1]) + (parts[2] + parts[3])


def pair_times(a, b):
    return (a[0] * b[0] - a[1] * b[1], a[0] * b[1] + a[1] * b[0])


def pair_times_conj(a, b):
    return (a[0] * b[0] + a[1] * b[1], a[1] * b[0] - a[0] * b[1])


def pair_conj_times(a, b):
    return (a[0] * b[0] + a[1] * b[1], a[0] * b[1] - a[1] * b[0])


def pair_add(a, b):
    return (a[0] + b[0], a[1] + b[1])


def matrix(parts):
    return [[(parts[0], parts[1]), (parts[2], parts[3])], [(parts[4], parts[5]), (parts[6], parts[7])]]


def flat(m):
    return [m[0][0][0], m[0][0][1], m[0][1][0], m[0][1][1], m[1][0][0], m[1][0][1], m[1][1][0], m[1][1][1]]


def times(a, b):
    return [[pair_add(pair_times(a[i][0], b[0][j]), pair_times(a[i][1], b[1][j])) for j in range(2)] for i in range(2)]


def times_h(a, b):
    return [
        [pair_add(pair_times_conj(a[i][0], b[j][0]), pair_times_conj(a[i][1], b[j][1])) for j in range(2)]
        for i in range(2)
    ]


def h_times(a, b):
    return [
        [pair_add(pair_conj_times(a[0][i], b[0][j]), pair_conj_times(a[1][i], b[1][j])) for j in range(2)]
        for i in range(2)
    ]


def split(value):
    high = value.astype(bf16)
    return high, (value - high.astype(f32)).astype(bf16)


VMEM = pl.BlockSpec(memory_space=pltpu.VMEM)


def call(body, outs, scratch, args, aliases=None, smem=0):
    return pl.pallas_call(
        body,
        out_shape=[jax.ShapeDtypeStruct(*o) for o in outs],
        in_specs=[pl.BlockSpec(memory_space=pltpu.SMEM)] * smem + [VMEM] * (len(args) - smem),
        out_specs=[VMEM] * len(outs),
        scratch_shapes=[pltpu.VMEM(*b) for b in scratch],
        compiler_params=pltpu.CompilerParams(vmem_limit_bytes=28 << 20),
        input_output_aliases=aliases or {},
    )(*args)


def join_kernel(a, b, c, d, out):
    for i, ref in enumerate((a, b, c, d)):
        out[i * 64 : i * 64 + 64, :] = ref[...]


def last_kernel(degrees, near0, near1, near2, near3, basis, current, dual, rho, out, dual_out, poly):
    fitted = None
    for j in range(degrees):
        sums = []
        for half in range(2):
            rows = slice(half * 64, half * 64 + 64)
            terms = [
                basis[half * 4 + d : half * 4 + d + 1, j : j + 1] * ref[rows, :]
                for d, ref in enumerate((near0, near1, near2, near3))
            ]
            sums.append((terms[0] + terms[1]) + (terms[2] + terms[3]))
        coefficient = sums[0] + sums[1]
        poly[j * 64 : j * 64 + 64, :] = coefficient
        term = basis[0:1, j : j + 1] * coefficient
        fitted = term if fitted is None else fitted + term
    out[...] = current[...]
    dual_out[...] = dual[...] + rho[...] * (current[...] - fitted)


def step_kernel(count, zh, squares, value, down, far_value, far_down, current, pair, out):
    owner = lax.broadcasted_iota(jnp.int32, (64, 128), 0) & 1
    steps = []
    for side in (zh[0], 1 - zh[0]):
        kept = jnp.where(owner == side, squares[...], 0.0)
        total = jnp.sum(jnp.sum(kept, axis=0, keepdims=True), axis=1, keepdims=True)
        steps.append(step_size / jnp.sqrt(total / count + epsilon))
    pair[0:64, :] = value[...] - steps[0] * down[...]
    pair[64:128, :] = far_value[...] - steps[1] * far_down[...]
    out[...] = current[...] - steps[0] * down[...]


def stations_of(sky):
    rows = sky[128:144, :].astype(f32)
    return [rows[2 * side : 2 * side + 1] * 16.0 + rows[2 * side + 1 : 2 * side + 2] for side in range(2)]


def place_table_kernel(sky0, sky1, sky2, sky3, after, out):
    station = lax.broadcasted_iota(jnp.int32, (512, 512), 1).astype(f32)
    rows = [row for sky in (sky0, sky1, sky2, sky3) for row in stations_of(sky)]
    columns = jnp.concatenate(rows, axis=0).T
    for j in range(8):
        hit = station == columns[:, j : j + 1]
        out[j * 512 : j * 512 + 512, :] = jnp.where(hit, 1.0, 0.0).astype(bf16)


def sky_kernel(tm, coherency, stations, *outs):
    slot = lax.broadcasted_iota(jnp.int32, (64, 64), 0)
    owner = tm[0] ^ ((slot & 3) * 8 + (slot >> 4) * 2 + ((slot >> 2) & 1))
    order = owner * 2 + ((slot >> 3) & 1) == lax.broadcasted_iota(jnp.int32, (64, 64), 1)
    order = jnp.where(order, 1.0, 0.0).astype(bf16)
    for c in range(8):
        rows = jnp.dot(order, coherency[c], preferred_element_type=f32).astype(bf16)
        for d in range(4):
            outs[d][c * 16 : c * 16 + 16, :] = rows[d * 16 : d * 16 + 16, :]
    ids = stations[...]
    parts = [part for side in range(2) for part in (ids[side : side + 1] >> 4, ids[side : side + 1] & 15)]
    rows = jnp.concatenate(parts + [jnp.zeros((12, 512), jnp.int32)], axis=0).astype(f32).astype(bf16)
    for d in range(4):
        outs[d][128:144, :] = rows


def pick_kernel(own, other, sky0, sky1, sky2, sky3, gains, stage, lhs, table):
    stage[0:256, :] = own[...]
    stage[256:512, :] = other[...]
    for c in range(8):
        for block in range(4):
            first = stage[pl.ds(block * 8 + c, 8, stride=64), :]
            second = stage[pl.ds(block * 8 + 32 + c, 8, stride=64), :]
            high, low = split(jnp.concatenate([first, second], axis=0))
            lanes = slice(block * 128, block * 128 + 128)
            lhs[c * 16 : c * 16 + 16, lanes] = high
            lhs[128 + c * 16 : 144 + c * 16, lanes] = low
    station = lax.broadcasted_iota(jnp.int32, (512, 512), 0).astype(f32)
    for s, sky in enumerate((sky0, sky1, sky2, sky3)):
        for side, row in enumerate(stations_of(sky)):
            hit = station == row
            table[s % 2, :, side * 512 : side * 512 + 512] = jnp.where(hit, 1.0, 0.0).astype(bf16)
        both = jnp.dot(lhs[...], table[s % 2], preferred_element_type=f32)
        gains[:, s * 1024 : s * 1024 + 1024] = both[0:128] + both[128:256]


def halves(ref, c, lanes):
    rows = ref[c * 16 : c * 16 + 16, lanes].astype(f32)
    return rows[0:8], rows[8:16]


def model_kernel(count, moved, *refs):
    if moved:
        before, delta, n0, n1, n2, n3, sky0, sky1, sky2, sky3, vis, gains, part, rate = refs
        total = (n0[...] + n1[...]) + (n2[...] + n3[...])
        mean = jnp.sum(total, axis=(0, 1), keepdims=True) / count
        step = jnp.broadcast_to(step_size / jnp.sqrt(mean + epsilon), (8, 128))
        rate[...] = step
    else:
        gains, sky0, sky1, sky2, sky3, vis, part = refs
    for s, sky in enumerate((sky0, sky1, sky2, sky3)):

        def block(nb, carry, s=s, sky=sky):
            def at(base):
                return pl.ds(pl.multiple_of(base + nb * 128, 128), 128)

            here, plane, qlane = at(0), at(s * 1024), at(s * 1024 + 512)
            models = [halves(sky, c, here) for c in range(8)]
            sums = None
            for h in range(2):
                ends = []
                for lanes in (plane, qlane):
                    values = []
                    for c in range(8):
                        rows = slice(c * 16 + h * 8, c * 16 + h * 8 + 8)
                        if moved:
                            value = before[rows, lanes] - step * delta[rows, lanes]
                            gains[rows, lanes] = value
                        else:
                            value = gains[rows, lanes]
                        values.append(value)
                    ends.append(matrix(values))
                product = times(ends[0], matrix([m[h] for m in models]))
                result = flat(times_h(product, ends[1]))
                sums = result if sums is None else [a + b for a, b in zip(sums, result)]
            for c in range(8):
                row = jnp.sum(sums[c], axis=0, keepdims=True)
                if s == 0:
                    row = row - vis[c : c + 1, here]
                part[s * 8 + c : s * 8 + c + 1, here] = row
            return carry

        lax.fori_loop(0, 4, block, 0)


def terms_kernel(weight, part, r1, r2, r3, gains, sky0, sky1, sky2, sky3, place, gown, gother, terms, stage):
    for s, sky in enumerate((sky0, sky1, sky2, sky3)):

        def block(nb, carry, s=s, sky=sky):
            def at(base):
                return pl.ds(pl.multiple_of(base + nb * 128, 128), 128)

            def slot(ref, t):
                return ref[t * 8 : t * 8 + 8, at(0)]

            error = (slot(part, s) + slot(r1, s ^ 1)) + (slot(r2, s ^ 2) + slot(r3, s ^ 3))
            error = error * weight
            errors = matrix([jnp.broadcast_to(error[c : c + 1], (8, 128)) for c in range(8)])
            models = [halves(sky, c, at(0)) for c in range(8)]
            outs = ([], [])
            for h in range(2):
                rows = [slice(c * 16 + h * 8, c * 16 + h * 8 + 8) for c in range(8)]
                model = matrix([m[h] for m in models])
                second = matrix([gains[r, at(s * 1024 + 512)] for r in rows])
                outs[0].append(flat(times(errors, times_h(second, model))))
                first = matrix([gains[r, at(s * 1024)] for r in rows])
                outs[1].append(flat(h_times(errors, times(first, model))))
            for side in range(2):
                lanes = at(s * 1024 + side * 512)
                for c in range(8):
                    high, low = split(jnp.concatenate([outs[side][0][c], outs[side][1][c]], axis=0))
                    terms[c * 16 : c * 16 + 16, lanes] = high
                    terms[128 + c * 16 : 144 + c * 16, lanes] = low
            return carry

        lax.fori_loop(0, 4, block, 0)
    both = jnp.dot(terms[...], place[...], preferred_element_type=f32)
    sums = both[0:128] + both[128:256]
    for c in range(8):
        for block in range(8):
            row = c * 16 + block // 4 * 8
            lane = block % 4 * 128
            stage[pl.ds(block * 8 + c, 8, stride=64), :] = sums[row : row + 8, lane : lane + 128]
    gown[...] = stage[0:256, :]
    gother[...] = stage[256:512, :]


def body(visibilities, coherency, stations, jones, dual, cluster, rho_table):
    channels = lax.axis_size("zh") * lax.axis_size("y")
    degrees = min(3, channels - 1)
    tm = lax.axis_index("tm")
    zh = lax.axis_index("zh")
    freq = zh * 4 + lax.axis_index("y")
    weight = np.float32(math.sqrt(S / (2.0 * lax.axis_size("tm") * visibilities.shape[3])))
    count = 8.0 * K * S

    def packed(value):
        return value.reshape(8, 8, 128).transpose(1, 0, 2).reshape(64, 128)

    def unpacked(value):
        return value.reshape(-1, 8, 8, 128).transpose(0, 2, 1, 3).reshape(-1, 8, 1024)

    start = packed(jones[0])
    dual_start = packed(dual[0])
    rho_dir = jnp.sum(
        jnp.where(cluster[:, None] == jnp.arange(rho_table.shape[0], dtype=jnp.int32)[None, :], rho_table[None, :], 0.0),
        axis=1,
    )
    rho = jnp.repeat(lax.dynamic_slice_in_dim(rho_dir, tm * 2, 2), 32)[:, None]
    table = poly_basis(channels, degrees)
    wide = np.zeros((channels, 8, 128), np.float32)
    for f in range(channels):
        wide[f, :, :degrees] = [table[f ^ d] for d in range(8)]
    rows = lax.dynamic_index_in_dim(jnp.asarray(wide), freq, 0, keepdims=False)
    basis = [rows[d, :degrees] for d in range(8)]

    def y_line(value):
        return [value] + [swap(value, "y", d) for d in (1, 2, 3)]

    def consensus_of(value):
        pair = jnp.stack([value, swap(value, "zh", 1)])
        parts = y_line(pair)
        sums = []
        for half in range(2):
            rows = basis[half * 4 : half * 4 + 4]
            terms = [b.reshape((-1,) + (1,) * value.ndim) * v[half][None] for b, v in zip(rows, parts)]
            sums.append((terms[0] + terms[1]) + (terms[2] + terms[3]))
        return sums[0] + sums[1]

    def project(poly):
        return jnp.sum(basis[0][:, None, None] * poly, axis=0)

    own, other = spread(start)
    args = (tm.astype(jnp.int32).reshape(1), coherency[0, 0], stations[0])
    skies = call(sky_kernel, [((144, 512), bf16)] * 4, [], args, smem=1)
    skies = [skies[0]] + [swap(skies[d], "tm", 2 * d) for d in (1, 2, 3)]
    vis = visibilities[0, 0]
    many = ((128, 4096), f32)
    model_outs = [((32, 512), f32)]

    def gains_of(own, other):
        scratch = [((512, 128), f32), ((256, 512), bf16), ((2, 512, 1024), bf16)]
        return call(pick_kernel, [many], scratch, (own, other, *skies))[0]

    def gradient_of(gains, part):
        others = [swap(part, "tm", 2 * d) for d in (1, 2, 3)]
        outs = [((256, 128), f32)] * 2
        scratch = [((256, 4096), bf16), ((512, 128), f32)]
        place = call(place_table_kernel, [((4096, 512), bf16)], [], (*skies, part))[0]
        args = (part, *others, gains, *skies, place)
        return collect(*call(functools.partial(terms_kernel, weight), outs, scratch, args))

    gains = gains_of(own, other)
    (part,) = call(functools.partial(model_kernel, count, False), model_outs, [], (gains, *skies, vis))

    fitted = project(consensus_of(start + dual_start / rho))
    descent = gradient_of(gains, part) + dual_start + rho * (start - fitted)

    down, dother = spread(descent)
    norm = jnp.sum((down * down + dother * dother).reshape(32, 8, 128), axis=0)
    norms = [norm] + [swap(norm, "tm", 2 * d) for d in (1, 2, 3)]
    delta = gains_of(down, dother)
    gains, part, rate = call(
        functools.partial(model_kernel, count, True),
        [many] + model_outs + [((8, 128), f32)],
        [],
        (gains, delta, *norms, *skies, vis),
        {0: 0},
    )
    current = start - rate[0:1, :] * descent
    fitted = project(consensus_of(current + dual_start / rho))
    dual_now = dual_start + rho * (current - fitted)

    descent = gradient_of(gains, part) + dual_now + rho * (current - fitted)
    near = jnp.stack([current + dual_now / rho, descent])
    far = swap(near, "zh", 1)
    squares = jnp.broadcast_to(jnp.sum(descent * descent, axis=0, keepdims=True), (64, 128))
    squares = lax.optimization_barrier(squares).reshape(64, 1, 128)
    squares = lax.all_to_all(squares, ("tm", "zh"), 0, 0, tiled=True).reshape(64, 128)
    args = (zh.astype(jnp.int32).reshape(1), squares, near[0], near[1], far[0], far[1], current)
    outs = [((128, 128), f32), ((64, 128), f32)]
    pair, current = call(functools.partial(step_kernel, count), outs, [], args, smem=1)
    lines = y_line(pair)
    args = (*lines, rows, current, dual_now, jnp.broadcast_to(rho, (64, 128)))
    outs = [((64, 128), f32), ((64, 128), f32), ((degrees * 64, 128), f32)]
    current, dual_now, poly = call(functools.partial(last_kernel, degrees), outs, [], args)
    return unpacked(current), unpacked(dual_now), unpacked(poly)


def solution(mesh):
    fine = Mesh(mesh.devices.reshape(32, 2, 4), ("tm", "zh", "y"))
    freq = ("zh", "y")

    return jax.shard_map(
        body,
        mesh=fine,
        in_specs=(
            P("tm", freq, None, None),
            P("tm", freq, None, None, None),
            P("tm", None, None),
            P(freq, None, "tm"),
            P(freq, None, "tm"),
            P(),
            P(),
        ),
        out_specs=(P(freq, None, "tm"), P(freq, None, "tm"), P(None, None, "tm")),
        check_vma=False,
    )
```
